256 devices in a mesh: dp: 16 (over x_lo, z), tensor: 16 (over y, x_hi, core).
Axes of the slice: x: 4 (x_hi: 2, x_lo: 2; x = x_hi * 2 + x_lo), y: 4, z: 8, core: 2. Of those that a mesh axis runs over, the one named last changes fastest.
Arguments:
- query_rows: bfloat16 [32768, 8192], P('dp', 'tensor'), may hold values from -16 to 16
- key_rows: bfloat16 [32768, 1024], P('dp'), may hold values from -10 to 10
- value_rows: bfloat16 [32768, 1024], P('dp'), may hold values from -600 to 600
- segment_ids: int32 [32768], P('dp'), may hold values from 0 to 127, never falling along the last dimension, each value on 1 to 512 neighbouring positions
- norm_gain: float32 [8192], replicated, may hold values from 0.1 to 1.9
- draft_weight: bfloat16 [8192, 512], P('tensor', 'dp'), may hold values from -0.0625 to 0.0625
- targets: bfloat16 [32768, 512], P(('dp', 'tensor')), may hold values from -6 to 6
Outputs:
- grad_weight: float32 [8192, 512], P('tensor', 'dp')
The draws below stay inside these ranges and needn't reach their ends.
Inputs may be any that keep to these rules, and one draw needn't show every extreme that they name: `segment_ids`: document ids never fall along the tokens; a document has at most 512 tokens, and one has exactly 512.
All inputs are finite; a program needn't handle non-finite values.
Results may differ from the reference program's by a relative error of at most 0.0015.
Values may be sent and summed in bfloat16 or wider, within the bound.
No kernel may reach another device: no remote copies, remote signals or barrier semaphores. Data moves between devices by JAX's collectives and lax.ppermute only.
A program may use at most 128 MiB of HBM per device.

```python
import math
import jax
import jax.numpy as jnp
import numpy as np
from jax import lax

D = 8192
HEADS = 64
KV_HEADS = 8
HEAD_DIM = 128
KEY_OUT = 512
SEQ = 2048
DOC_MAX = 512
TOKENS = 32768
DOCS = 128


def draw_key_rows(key, part):
    noise = jnp.clip(jax.random.normal(jax.random.fold_in(key, 1), (TOKENS, KV_HEADS * HEAD_DIM), jnp.float32), -6.0, 6.0)
    return noise.astype(jnp.bfloat16)


def draw_query_rows(key, part):
    noise = jnp.clip(jax.random.normal(jax.random.fold_in(key, 2), (TOKENS, HEADS * HEAD_DIM), jnp.float32), -6.0, 6.0)
    return noise.astype(jnp.bfloat16)


def draw_value_rows(key, part):
    columns = jnp.arange(KV_HEADS * HEAD_DIM)
    shared_of = (columns // HEAD_DIM).astype(jnp.float32)
    row_scale = jnp.exp(jax.random.uniform(jax.random.fold_in(key, 4), (TOKENS, 1), jnp.float32, 0.0, 2.302585))
    noise = jnp.clip(jax.random.normal(jax.random.fold_in(key, 3), (TOKENS, KV_HEADS * HEAD_DIM), jnp.float32), -6.0, 6.0)
    column_scale = 10.0 ** (shared_of / (KV_HEADS - 1))
    return (noise * column_scale[None, :] * row_scale).astype(jnp.bfloat16)


def level_of(stream_key, extent, split, low, high):
    def one(axis_at, blocks):
        draws = jax.random.uniform(jax.random.fold_in(jax.random.fold_in(stream_key, 6), axis_at), (blocks,), jnp.float32, low / len(split), high / len(split))
        return jnp.repeat(jnp.exp(draws), extent[axis_at] // blocks).reshape((-1,) + (1,) * (len(extent) - axis_at - 1))

    factor_of = one(*split[0])
    for cut in split[1:]:
        factor_of = factor_of * one(*cut)
    return factor_of


def split_up(number_of, total, reach, lean):
    weights = [(1 << 20) // math.isqrt(standing ** lean) + 1 for standing in range(2, number_of + 1)]
    surplus, counts = total - reach - (number_of - 1), [1] * (number_of - 1)
    while surplus > 0:
        movable = [i for i in range(number_of - 1) if counts[i] < reach]
        mass, left = sum([weights[i] for i in movable]), surplus
        for i in movable:
            more = min(reach - counts[i], max(1, left * weights[i] // mass), surplus)
            counts[i] = counts[i] + more
            surplus = surplus - more
    return np.array([reach] + counts)


def uneven_parts(own_key, count, total, bound, skew):
    if count == 2:
        one = jax.random.randint(own_key, (), max(1, total - bound), min(bound, total - 1) + 1)
        return jnp.stack([one, total - one])
    lengths = jnp.asarray(split_up(count, total, bound, skew), jnp.int32)
    pairs = (count - 1) // 2
    donor, taker = lengths[1:1 + 2 * pairs:2], lengths[2:2 + 2 * pairs:2]
    room = jnp.minimum(donor - 1, bound - taker)
    moved = jax.random.randint(jax.random.fold_in(own_key, 1), (pairs,), 0, 1 << 20) % (room + 1)
    lengths = lengths.at[1:1 + 2 * pairs:2].set(donor - moved).at[2:2 + 2 * pairs:2].set(taker + moved)
    return lengths[jax.random.permutation(jax.random.fold_in(own_key, 2), count)]


def normal_values(key, dims, spread, most, pieces=(), held_as=jnp.bfloat16):
    result = jax.random.normal(key, dims, jnp.float32) * spread
    if len(pieces) > 0:
        result = level_of(key, dims, pieces, -0.22, 0.18) * result
    return jnp.clip(result, min=-most, max=most).astype(held_as)


def setup_inputs(seed: int = 0) -> dict:
    seeds = jax.random.split(jax.random.key(seed), 8)
    return {
        "query_rows": draw_query_rows(jax.random.fold_in(seeds[7], 71), 0),
        "key_rows": draw_key_rows(jax.random.fold_in(seeds[7], 71), 0),
        "value_rows": draw_value_rows(jax.random.fold_in(seeds[7], 71), 0),
        "segment_ids": jnp.searchsorted(jnp.cumsum(uneven_parts(seeds[3], DOCS, TOKENS, DOC_MAX, 2)), jnp.arange(TOKENS), side="right").astype(jnp.int32),
        "norm_gain": jnp.clip(1.0 + 0.18 * jax.random.normal(seeds[4], (D,), jnp.float32), 0.1, 1.9),
        "draft_weight": normal_values(seeds[5], (D, KEY_OUT), D ** -0.5, 0.0625, ((0, 16), (1, 16))),
        "targets": normal_values(seeds[6], (TOKENS, KEY_OUT), 1.0, 6.0, ((0, 256),)),
    }


def attend_group(query_rows, key_rows, value_rows, segments):
    group = HEADS // KV_HEADS
    scale = HEAD_DIM ** (-0.5)
    length = query_rows.shape[0]
    places = jnp.arange(length, dtype=jnp.int32)
    allowed = (segments[:, None] == segments[None, :]) & (places[:, None] >= places[None, :])
    query_heads = query_rows.astype(jnp.float32).reshape(length, KV_HEADS, group, HEAD_DIM).transpose(1, 0, 2, 3)
    key_heads = key_rows.astype(jnp.float32).reshape(length, KV_HEADS, HEAD_DIM).transpose(1, 0, 2)
    value_heads = value_rows.astype(jnp.float32).reshape(length, KV_HEADS, HEAD_DIM).transpose(1, 0, 2)

    def one_head(operands):
        query_part, key_part, value_part = operands
        scores = jnp.einsum('qrd,kd->rqk', query_part, key_part) * scale
        scores = jnp.where(allowed[None], scores, -1e+30)
        shifted = jnp.exp(scores - lax.optimization_barrier(jnp.max(scores, axis=-1, keepdims=True)))
        probs = (shifted / lax.optimization_barrier(jnp.sum(shifted, axis=-1, keepdims=True))).astype(jnp.bfloat16)
        probs = lax.optimization_barrier(probs)
        mixed = jnp.einsum('rqk,kd->qrd', probs.astype(jnp.float32), value_part)
        return mixed.astype(jnp.bfloat16)
    outputs = lax.map(one_head, (query_heads, key_heads, value_heads))
    return outputs.transpose(1, 0, 2, 3).reshape(length, KV_HEADS * group * HEAD_DIM)

def reference(query_rows, key_rows, value_rows, segment_ids, norm_gain, draft_weight, targets):
    total_tokens = query_rows.shape[0]
    groups = total_tokens // SEQ

    def per_group(number):
        offset = number * SEQ
        return attend_group(lax.dynamic_slice_in_dim(query_rows, offset, SEQ, 0), lax.dynamic_slice_in_dim(key_rows, offset, SEQ, 0), lax.dynamic_slice_in_dim(value_rows, offset, SEQ, 0), lax.dynamic_slice_in_dim(segment_ids, offset, SEQ, 0))
    attended = lax.map(per_group, jnp.arange(groups, dtype=jnp.int32)).reshape(total_tokens, D)
    attended = lax.optimization_barrier(attended)
    features = attended.astype(jnp.float32)
    mean_square = lax.optimization_barrier(jnp.mean(features * features, axis=-1, keepdims=True))
    normed = (features * lax.rsqrt(mean_square + 1e-06) * norm_gain[None, :]).astype(jnp.bfloat16)
    predicted = jnp.dot(normed, draft_weight, preferred_element_type=jnp.float32)
    residual = predicted - targets.astype(jnp.float32)
    grad_pred = (jnp.clip(residual, -1.0, 1.0) / jnp.sqrt(jnp.float32(total_tokens))).astype(jnp.bfloat16)
    return jnp.dot(normed.T, grad_pred, preferred_element_type=jnp.float32)
```

```python
import math

import jax
import jax.numpy as jnp
from jax import lax
from jax.experimental import pallas as pl
from jax.experimental.pallas import tpu as pltpu
from jax.sharding import PartitionSpec as P

HEADS = 64
KV_HEADS = 8
HEAD_DIM = 128
DOC_MAX = 512
BLOCK = 128
EXTRA = 16
BF16 = jnp.bfloat16
F32 = jnp.float32
F16 = jnp.float16
ROOT_SCALE = 2.0**20


def scalar_rows(x):
    rows = lax.broadcasted_iota(jnp.int32, (EXTRA, BLOCK), 0)
    high = x.astype(BF16).astype(F32)
    rest = x - high
    middle = rest.astype(BF16).astype(F32)
    low = rest - middle
    return jnp.where(
        rows == 0, high, jnp.where(rows == 1, middle, jnp.where(rows == 2, low, 0.0))
    ).astype(BF16)


def scalar_of(rows):
    return jnp.sum(rows.astype(F32), axis=0, keepdims=True)


def attention(
    places, segment_ids, first, count, query_rows, key_rows, value_rows, segments,
    weight=None, gains=None,
):
    length, width = query_rows.shape
    heads = width // HEAD_DIM
    blocks = length // BLOCK
    most = min(blocks, DOC_MAX // BLOCK + 1)
    step = math.log2(math.e) * HEAD_DIM ** (-0.5)

    def body(place, ids, *refs):
        query, key, value, segment = refs[:4]
        out, square = refs[-2:] if weight is None else refs[-3:-1]
        block = (first + pl.program_id(0)) * 2 + place[0]
        needed = 1
        for back in range(1, most):
            end = jnp.maximum((block - back) * BLOCK + BLOCK - 1, 0)
            reached = (block >= back) & (ids[end] == ids[block * BLOCK])
            needed = needed + reached.astype(jnp.int32)

        def over(near):
            window = near * BLOCK
            begin = jnp.maximum(block + 1 - near, 0)
            start = pl.multiple_of(begin * BLOCK, BLOCK)
            shape = (BLOCK, BLOCK)
            diagonal = lax.broadcasted_iota(jnp.int32, shape, 0) == lax.broadcasted_iota(
                jnp.int32, shape, 1
            )
            ones = jnp.ones(shape, BF16)
            columns = [
                jnp.dot(
                    jnp.where(diagonal, segment[pl.ds(begin + n, 1), :], 0)
                    .astype(F32).astype(BF16),
                    ones, preferred_element_type=F32,
                )
                for n in range(near)
            ]
            key_at = start + lax.broadcasted_iota(jnp.int32, (window, BLOCK), 0)
            query_at = block * BLOCK + lax.broadcasted_iota(jnp.int32, (window, BLOCK), 1)
            mine = segment[pl.ds(block, 1), :].astype(F32)
            same = jnp.concatenate(columns, axis=0) == mine
            bias = jnp.where(same & (key_at <= query_at), 0.0, -1e30)
            stacked = jnp.concatenate(
                [query[:, h * HEAD_DIM : (h + 1) * HEAD_DIM] for h in range(heads)], axis=0
            )
            scores = lax.dot_general(
                key[pl.ds(start, window), :], stacked, (((1,), (1,)), ((), ())),
                preferred_element_type=F32,
            )
            scores = scores + jnp.concatenate([bias] * heads, axis=1)
            top = jnp.max(scores, axis=0, keepdims=True)
            shifted = jnp.exp2((scores - top) * step)
            inverse = 1.0 / jnp.sum(shifted, axis=0, keepdims=True)
            probs = (shifted * inverse).astype(BF16)
            mixed = lax.dot_general(
                value[pl.ds(start, window), :], probs, (((0,), (0,)), ((), ())),
                preferred_element_type=F32,
            ).astype(BF16)
            for h in range(heads):
                out[0, h * HEAD_DIM : (h + 1) * HEAD_DIM, :] = mixed[:, h * BLOCK : (h + 1) * BLOCK]

        below = 0
        for near in range(2, most + 1):
            fits = (needed <= near) & (needed > below) if near < most else needed > below
            pl.when(fits)(lambda near=near: over(near))
            below = near

        wide = out[0].astype(F32)
        total = jnp.sum(wide * wide, axis=0, keepdims=True)
        square[0] = jnp.broadcast_to(total, (8, BLOCK))
        if weight is not None:
            mat, gain, share = refs[4], refs[5], refs[-1]
            outs = mat.shape[0]
            share[0, 0:outs, :] = jnp.dot(
                mat[...], (wide * gain[...]).astype(BF16), preferred_element_type=F32
            )
            share[0, outs : outs + EXTRA, :] = jnp.broadcast_to(total, (EXTRA, BLOCK))

    in_specs = [
        pl.BlockSpec((BLOCK, width), lambda i, s, d: ((first + i) * 2 + s[0], 0)),
        pl.BlockSpec((length, HEAD_DIM), lambda i, s, d: (0, s[1])),
        pl.BlockSpec((length, HEAD_DIM), lambda i, s, d: (0, s[1])),
        pl.BlockSpec((blocks, BLOCK), lambda i, s, d: (0, 0)),
    ]
    out_specs = [
        pl.BlockSpec((1, width, BLOCK), lambda i, s, d: (i, 0, 0)),
        pl.BlockSpec((1, 8, BLOCK), lambda i, s, d: (i, 0, 0)),
    ]
    out_shape = [
        jax.ShapeDtypeStruct((count, width, BLOCK), BF16),
        jax.ShapeDtypeStruct((count, 8, BLOCK), F32),
    ]
    operands = [query_rows, key_rows, value_rows, segments]
    if weight is not None:
        outs = weight.shape[0]
        in_specs += [
            pl.BlockSpec((outs, width), lambda i, s, d: (0, 0)),
            pl.BlockSpec((width, BLOCK), lambda i, s, d: (0, 0)),
        ]
        operands += [weight, gains]
        out_specs.append(pl.BlockSpec((1, outs + EXTRA, BLOCK), lambda i, s, d: (i, 0, 0)))
        out_shape.append(jax.ShapeDtypeStruct((count, outs + EXTRA, BLOCK), F32))
    grid = pltpu.PrefetchScalarGridSpec(
        num_scalar_prefetch=2, grid=(count,), in_specs=in_specs, out_specs=out_specs
    )
    return pl.pallas_call(body, grid_spec=grid, out_shape=out_shape, name="attention")(
        places, segment_ids, *operands
    )


IN_VMEM = pl.BlockSpec(memory_space=pltpu.VMEM)


def project(attended, squares, weight, gains):
    outs = weight.shape[0]
    rows = outs + EXTRA
    pieces = len(attended)
    count = sum(x.shape[0] for x in attended)

    def body(*refs):
        mat, gain, out = refs[2 * pieces], refs[2 * pieces + 1], refs[-1]
        at = 0
        for att, sq in zip(refs[:pieces], refs[pieces : 2 * pieces]):
            number = att.shape[0]
            wide = jnp.concatenate(
                [(att[u].astype(F32) * gain[...]).astype(BF16) for u in range(number)], axis=1
            )
            sums = jnp.dot(mat[...], wide, preferred_element_type=F32)
            for u in range(number):
                out[at + u, 0:outs, :] = sums[:, u * BLOCK : (u + 1) * BLOCK].astype(BF16)
                out[at + u, outs:rows, :] = scalar_rows(sq[u, 0:1, :])
            at = at + number

    operands = list(attended) + list(squares) + [weight, gains]
    return pl.pallas_call(
        body,
        in_specs=[IN_VMEM] * len(operands),
        out_specs=IN_VMEM,
        out_shape=jax.ShapeDtypeStruct((count, rows, BLOCK), BF16),
        name="project",
    )(*operands)


def together(own, other):
    count, rows, _ = own.shape
    outs = rows - EXTRA

    def body(left, right, out):
        for u in range(count // 2):
            out[u, 0:outs, :] = (
                left[u, 0:outs, :] + right[u, 0:outs, :].astype(F32)
            ).astype(BF16)
            total = left[u, outs : outs + 1, :] + scalar_of(right[u, outs:rows, :])
            out[u, outs:rows, :] = scalar_rows(total)

    spec = pl.BlockSpec((count // 2, rows, BLOCK), lambda i: (i, 0, 0))
    return pl.pallas_call(
        body,
        grid=(2,),
        in_specs=[spec, spec],
        out_specs=spec,
        out_shape=jax.ShapeDtypeStruct(other.shape, BF16),
        name="together",
    )(own, other)


def derive(parts, targets, features, total_tokens):
    count, rows, _ = parts.shape
    outs = rows - EXTRA
    root = math.sqrt(total_tokens)

    def body(got, want, out):
        total = jnp.zeros((1, BLOCK), F32)
        sums = jnp.zeros((outs, BLOCK), F32)
        for u in range(count):
            total = total + scalar_of(got[u, outs:rows, :])
            sums = sums + got[u, 0:outs, :].astype(F32)
        factor = lax.rsqrt(total / features + 1e-06)
        residual = sums * factor - want[...].astype(F32).T
        slope = (jnp.clip(residual, -1.0, 1.0) / root).astype(BF16)
        extra = scalar_rows(factor)
        for u in range(count):
            out[u, 0:outs, :] = slope
            out[u, outs:rows, :] = extra

    return pl.pallas_call(
        body,
        in_specs=[IN_VMEM, IN_VMEM],
        out_specs=IN_VMEM,
        out_shape=jax.ShapeDtypeStruct(parts.shape, BF16),
        name="derive",
    )(parts, targets)


def gradient(slopes, attended, gains, before=None):
    count, rows, _ = slopes.shape
    outs = rows - EXTRA
    width = attended[0].shape[1]

    def body(*refs):
        slope, gain = refs[0], refs[1]
        out = refs[-1]
        normed = []
        for att in refs[2 : 2 + len(attended)]:
            for u in range(att.shape[0]):
                factor = scalar_of(slope[len(normed), outs:rows, :])
                normed.append((att[u].astype(F32) * factor * gain[...]).astype(BF16))
        left = jnp.concatenate([slope[u, 0:outs, :] for u in range(count)], axis=1)
        sums = lax.dot_general(
            left, jnp.concatenate(normed, axis=1), (((1,), (1,)), ((), ())),
            preferred_element_type=F32,
        )
        if before is None:
            out[...] = sums
        else:
            sums = sums + refs[-2][...]
            root = jnp.sqrt(jnp.abs(sums) * ROOT_SCALE)
            out[...] = jnp.where(sums < 0, -root, root)

    operands = [slopes, gains] + list(attended) + ([] if before is None else [before])
    return pl.pallas_call(
        body,
        in_specs=[IN_VMEM] * len(operands),
        out_specs=IN_VMEM,
        out_shape=jax.ShapeDtypeStruct((outs, width), F32),
        name="gradient",
    )(*operands)


def exchange(x, axis, bit):
    size = lax.axis_size(axis)
    return lax.ppermute(x, axis, [(i, i ^ bit) for i in range(size)])


def exchanges(x, low, high):
    return (
        x, exchange(x, "dp", low), exchange(x, "dp", high), exchange(x, "dp", low | high)
    )


def ordered(own, other, axis, bit):
    late = (lax.axis_index(axis) & bit) != 0
    return jnp.where(late, jnp.concatenate([other, own]), jnp.concatenate([own, other]))


def joined(pieces, low, high):
    own, first, second, both = pieces
    return ordered(ordered(own, first, "dp", low), ordered(second, both, "dp", low), "dp", high)


def on_device(query_rows, key_rows, value_rows, segment_ids, norm_gain, draft_weight, targets):
    length, width = query_rows.shape
    blocks = length // BLOCK
    devices = lax.axis_size("tensor")
    total_tokens = length * lax.axis_size("dp")
    place = lax.axis_index("tensor")
    core = place % 2
    chips = [[2 * k + c for k in range(devices // 2)] for c in range(2)]
    kv_head = place * (width // HEAD_DIM) // (HEADS // KV_HEADS)

    segments = segment_ids.reshape(blocks, BLOCK)
    gain = lax.dynamic_slice_in_dim(norm_gain, place * width, width, 0)
    gains = jnp.broadcast_to(gain[:, None], (width, BLOCK))

    def attend(parity, first, count, *more):
        places = jnp.stack([parity, kv_head]).astype(jnp.int32)
        return attention(
            places, segment_ids, first, count, query_rows, key_rows, value_rows, segments, *more
        )

    half = blocks // 2
    cuts = (0, half // 4, half - 3 * half // 8, half)
    round_one = exchanges(draft_weight.T[None], 1, 2)
    theirs_a = attend(1 - core, 0, cuts[1])
    round_one, theirs_a = lax.optimization_barrier((round_one, theirs_a))
    octet = joined(round_one, 1, 2)
    round_two = exchange(octet, "dp", 4)
    theirs_b = attend(1 - core, cuts[1], cuts[2] - cuts[1])
    octet, round_two, theirs_b = lax.optimization_barrier((octet, round_two, theirs_b))
    octet = ordered(octet, round_two, "dp", 4)
    round_three = exchange(octet, "dp", 8)
    theirs_c = attend(1 - core, cuts[2], half - cuts[2])
    octet, round_three, theirs_c = lax.optimization_barrier((octet, round_three, theirs_c))
    weight = ordered(octet, round_three, "dp", 8).reshape(-1, width)

    theirs, squares = zip(theirs_a, theirs_b, theirs_c)
    received = exchange(project(theirs, squares, weight, gains), "tensor", 1)
    mine, _, share = attend(core, 0, half, weight, gains)
    received, share = lax.optimization_barrier((received, share))
    parts = lax.all_to_all(
        together(share, received), "tensor", split_axis=0, concat_axis=0, tiled=True,
        axis_index_groups=chips,
    )
    copies = derive(parts, targets, norm_gain.shape[0], total_tokens)
    my_slopes = lax.all_to_all(
        copies, "tensor", split_axis=0, concat_axis=0, tiled=True, axis_index_groups=chips
    )
    their_slopes = exchange(my_slopes, "tensor", 1)
    partial = gradient(my_slopes, (mine,), gains)
    partial = gradient(their_slopes, theirs, gains, partial)
    shares = partial.reshape(lax.axis_size("dp"), -1, width).astype(F16)
    shares = lax.all_to_all(shares, "dp", split_axis=0, concat_axis=0, tiled=True).astype(F32)
    return jnp.sum(shares * jnp.abs(shares), axis=0).T * (1.0 / ROOT_SCALE)


def solution(mesh):
    placed = (
        P("dp", "tensor"),
        P("dp", None),
        P("dp", None),
        P("dp"),
        P(),
        P("tensor", "dp"),
        P(("dp", "tensor"), None),
    )
    return jax.shard_map(
        on_device, mesh=mesh, in_specs=placed, out_specs=P("tensor", "dp"), check_vma=False
    )
```

```python
import math

import jax
import jax.numpy as jnp
from jax import lax
from jax.experimental import pallas as pl
from jax.experimental.pallas import tpu as pltpu
from jax.sharding import PartitionSpec as P

HEADS = 64
KV_HEADS = 8
HEAD_DIM = 128
DOC_MAX = 512
BLOCK = 128
EXTRA = 16
BF16 = jnp.bfloat16
F32 = jnp.float32
F16 = jnp.float16
ROOT_SCALE = 2.0**20


ROOM = pltpu.CompilerParams(vmem_limit_bytes=24 << 20)
IN_VMEM = pl.BlockSpec(memory_space=pltpu.VMEM)


def in_vmem(*arrays):
    return [pltpu.with_memory_space_constraint(x, pltpu.VMEM) for x in arrays]


def scalar_rows(x):
    rows = lax.broadcasted_iota(jnp.int32, (EXTRA, BLOCK), 0)
    high = x.astype(BF16).astype(F32)
    rest = x - high
    middle = rest.astype(BF16).astype(F32)
    low = rest - middle
    return jnp.where(
        rows == 0, high, jnp.where(rows == 1, middle, jnp.where(rows == 2, low, 0.0))
    ).astype(BF16)


def scalar_of(rows):
    return jnp.sum(rows.astype(F32), axis=0, keepdims=True)


def attention(
    places, segment_ids, first, count, query_rows, keys, values, segments,
    weight=None, gains=None,
):
    length, width = query_rows.shape
    heads = width // HEAD_DIM
    blocks = length // BLOCK
    most = min(blocks, DOC_MAX // BLOCK + 1)
    step = math.log2(math.e) * HEAD_DIM ** (-0.5)

    def body(place, ids, *refs):
        query, key, value, segment = refs[:4]
        out, square = refs[-2:] if weight is None else refs[-3:-1]
        at = pl.program_id(0)
        block = (first + at) * 2 + place[0]
        needed = 1
        for back in range(1, most):
            end = jnp.maximum((block - back) * BLOCK + BLOCK - 1, 0)
            reached = (block >= back) & (ids[end] == ids[block * BLOCK])
            needed = needed + reached.astype(jnp.int32)

        def over(near):
            window = near * BLOCK
            begin = jnp.maximum(block + 1 - near, 0)
            start = pl.multiple_of(begin * BLOCK, BLOCK)
            shape = (BLOCK, BLOCK)
            diagonal = lax.broadcasted_iota(jnp.int32, shape, 0) == lax.broadcasted_iota(
                jnp.int32, shape, 1
            )
            ones = jnp.ones(shape, BF16)
            columns = [
                jnp.dot(
                    jnp.where(diagonal, segment[pl.ds(begin + n, 1), :], 0)
                    .astype(F32).astype(BF16),
                    ones, preferred_element_type=F32,
                )
                for n in range(near)
            ]
            key_at = start + lax.broadcasted_iota(jnp.int32, (window, BLOCK), 0)
            query_at = block * BLOCK + lax.broadcasted_iota(jnp.int32, (window, BLOCK), 1)
            mine = segment[pl.ds(block, 1), :].astype(F32)
            same = jnp.concatenate(columns, axis=0) == mine
            bias = jnp.where(same & (key_at <= query_at), 0.0, -1e30)
            stacked = jnp.concatenate(
                [query[:, h * HEAD_DIM : (h + 1) * HEAD_DIM] for h in range(heads)], axis=0
            )
            scores = lax.dot_general(
                key[pl.ds(start, window), :], stacked, (((1,), (1,)), ((), ())),
                preferred_element_type=F32,
            )
            scores = scores + jnp.concatenate([bias] * heads, axis=1)
            top = jnp.max(scores, axis=0, keepdims=True)
            shifted = jnp.exp2((scores - top) * step)
            inverse = 1.0 / jnp.sum(shifted, axis=0, keepdims=True)
            probs = (shifted * inverse).astype(BF16)
            mixed = lax.dot_general(
                value[pl.ds(start, window), :], probs, (((0,), (0,)), ((), ())),
                preferred_element_type=F32,
            ).astype(BF16)
            for h in range(heads):
                out[at, h * HEAD_DIM : (h + 1) * HEAD_DIM, :] = mixed[:, h * BLOCK : (h + 1) * BLOCK]

        below = 0
        for near in range(2, most + 1):
            fits = (needed <= near) & (needed > below) if near < most else needed > below
            pl.when(fits)(lambda near=near: over(near))
            below = near

        wide = out[at].astype(F32)
        total = jnp.sum(wide * wide, axis=0, keepdims=True)
        square[at] = jnp.broadcast_to(total, (8, BLOCK))
        if weight is not None:
            mat, gain, share = refs[4], refs[5], refs[-1]
            outs = mat.shape[0]
            share[at, 0:outs, :] = jnp.dot(
                mat[...], (wide * gain[...]).astype(BF16), preferred_element_type=F32
            )
            share[at, outs : outs + EXTRA, :] = jnp.broadcast_to(total, (EXTRA, BLOCK))

    in_specs = [pl.BlockSpec((BLOCK, width), lambda i, s, d: ((first + i) * 2 + s[0], 0))]
    out_shape = [
        pltpu.VMEM((count, width, BLOCK), BF16),
        pltpu.VMEM((count, 8, BLOCK), F32),
    ]
    operands = [query_rows, *in_vmem(keys, values), segments]
    if weight is not None:
        operands += in_vmem(weight, gains)
        out_shape.append(pltpu.VMEM((count, weight.shape[0] + EXTRA, BLOCK), F32))
    grid = pltpu.PrefetchScalarGridSpec(
        num_scalar_prefetch=2,
        grid=(count,),
        in_specs=in_specs + [IN_VMEM] * (len(operands) - 1),
        out_specs=[IN_VMEM] * len(out_shape),
    )
    return pl.pallas_call(body, grid_spec=grid, out_shape=out_shape, name="attention",
        compiler_params=ROOM,
    )(
        places, segment_ids, *operands
    )


def project(attended, squares, weight, gains):
    outs = weight.shape[0]
    rows = outs + EXTRA
    pieces = len(attended)
    count = sum(x.shape[0] for x in attended)

    def body(*refs):
        mat, gain, out = refs[2 * pieces], refs[2 * pieces + 1], refs[-1]
        at = 0
        for att, sq in zip(refs[:pieces], refs[pieces : 2 * pieces]):
            number = att.shape[0]
            wide = jnp.concatenate(
                [(att[u].astype(F32) * gain[...]).astype(BF16) for u in range(number)], axis=1
            )
            sums = jnp.dot(mat[...], wide, preferred_element_type=F32)
            for u in range(number):
                out[at + u, 0:outs, :] = sums[:, u * BLOCK : (u + 1) * BLOCK].astype(BF16)
                out[at + u, outs:rows, :] = scalar_rows(sq[u, 0:1, :])
            at = at + number

    operands = list(attended) + list(squares) + [weight, gains]
    return pl.pallas_call(
        body,
        in_specs=[IN_VMEM] * len(operands),
        out_specs=IN_VMEM,
        out_shape=pltpu.VMEM((count, rows, BLOCK), BF16),
        name="project",
        compiler_params=ROOM,
    )(*in_vmem(*operands))


def together(own, other):
    count, rows, _ = own.shape
    outs = rows - EXTRA

    def body(left, right, out):
        for u in range(count):
            out[u, 0:outs, :] = (
                left[u, 0:outs, :] + right[u, 0:outs, :].astype(F32)
            ).astype(BF16)
            total = left[u, outs : outs + 1, :] + scalar_of(right[u, outs:rows, :])
            out[u, outs:rows, :] = scalar_rows(total)

    return pl.pallas_call(
        body,
        in_specs=[IN_VMEM, IN_VMEM],
        out_specs=IN_VMEM,
        out_shape=pltpu.VMEM(other.shape, BF16),
        name="together",
        compiler_params=ROOM,
    )(*in_vmem(own, other))


def derive(parts, targets, features, total_tokens):
    count, rows, _ = parts.shape
    outs = rows - EXTRA
    root = math.sqrt(total_tokens)

    def body(got, want, out):
        total = jnp.zeros((1, BLOCK), F32)
        sums = jnp.zeros((outs, BLOCK), F32)
        for u in range(count):
            total = total + scalar_of(got[u, outs:rows, :])
            sums = sums + got[u, 0:outs, :].astype(F32)
        factor = lax.rsqrt(total / features + 1e-06)
        residual = sums * factor - want[...].astype(F32).T
        slope = (jnp.clip(residual, -1.0, 1.0) / root).astype(BF16)
        extra = scalar_rows(factor)
        for u in range(count):
            out[u, 0:outs, :] = slope
            out[u, outs:rows, :] = extra

    return pl.pallas_call(
        body,
        in_specs=[IN_VMEM, IN_VMEM],
        out_specs=IN_VMEM,
        out_shape=pltpu.VMEM(parts.shape, BF16),
        name="derive",
        compiler_params=ROOM,
    )(*in_vmem(parts, targets))


def gradient(slopes, attended, gains, before=None):
    count, rows, _ = slopes.shape
    outs = rows - EXTRA
    width = attended[0].shape[1]

    def body(*refs):
        slope, gain = refs[0], refs[1]
        out = refs[-1]
        normed = []
        for att in refs[2 : 2 + len(attended)]:
            for u in range(att.shape[0]):
                factor = scalar_of(slope[len(normed), outs:rows, :])
                normed.append((att[u].astype(F32) * factor * gain[...]).astype(BF16))
        left = jnp.concatenate([slope[u, 0:outs, :] for u in range(count)], axis=1)
        sums = lax.dot_general(
            left, jnp.concatenate(normed, axis=1), (((1,), (1,)), ((), ())),
            preferred_element_type=F32,
        )
        if before is None:
            out[...] = sums
        else:
            sums = sums + refs[-2][...]
            root = jnp.sqrt(jnp.abs(sums) * ROOT_SCALE)
            out[...] = jnp.where(sums < 0, -root, root)

    operands = [slopes, gains] + list(attended) + ([] if before is None else [before])
    return pl.pallas_call(
        body,
        in_specs=[IN_VMEM] * len(operands),
        out_specs=IN_VMEM,
        out_shape=pltpu.VMEM((outs, width), F32),
        name="gradient",
        compiler_params=ROOM,
    )(*in_vmem(*operands))


def exchange(x, axis, bit):
    size = lax.axis_size(axis)
    return lax.ppermute(x, axis, [(i, i ^ bit) for i in range(size)])


def exchanges(x, low, high):
    return (
        x, exchange(x, "dp", low), exchange(x, "dp", high), exchange(x, "dp", low | high)
    )


def ordered(own, other, axis, bit):
    late = (lax.axis_index(axis) & bit) != 0
    return jnp.where(late, jnp.concatenate([other, own]), jnp.concatenate([own, other]))


def joined(pieces, low, high):
    own, first, second, both = pieces
    return ordered(ordered(own, first, "dp", low), ordered(second, both, "dp", low), "dp", high)


def on_device(query_rows, key_rows, value_rows, segment_ids, norm_gain, draft_weight, targets):
    length, width = query_rows.shape
    blocks = length // BLOCK
    devices = lax.axis_size("tensor")
    total_tokens = length * lax.axis_size("dp")
    place = lax.axis_index("tensor")
    core = place % 2
    chips = [[2 * k + c for k in range(devices // 2)] for c in range(2)]
    kv_head = place * (width // HEAD_DIM) // (HEADS // KV_HEADS)

    segments = segment_ids.reshape(blocks, BLOCK)
    keys = lax.dynamic_slice_in_dim(key_rows, kv_head * HEAD_DIM, HEAD_DIM, 1)
    values = lax.dynamic_slice_in_dim(value_rows, kv_head * HEAD_DIM, HEAD_DIM, 1)
    gain = lax.dynamic_slice_in_dim(norm_gain, place * width, width, 0)
    gains = jnp.broadcast_to(gain[:, None], (width, BLOCK))

    def attend(parity, first, count, *more):
        places = parity.astype(jnp.int32).reshape(1)
        return attention(
            places, segment_ids, first, count, query_rows, keys, values, segments, *more
        )

    half = blocks // 2
    cuts = (0, half // 4, half - 3 * half // 8, half)
    round_one = exchanges(draft_weight.T[None], 1, 2)
    theirs_a = attend(1 - core, 0, cuts[1])
    round_one, theirs_a = lax.optimization_barrier((round_one, theirs_a))
    octet = joined(round_one, 1, 2)
    round_two = exchange(octet, "dp", 4)
    theirs_b = attend(1 - core, cuts[1], cuts[2] - cuts[1])
    octet, round_two, theirs_b = lax.optimization_barrier((octet, round_two, theirs_b))
    octet = ordered(octet, round_two, "dp", 4)
    round_three = exchange(octet, "dp", 8)
    theirs_c = attend(1 - core, cuts[2], half - cuts[2])
    octet, round_three, theirs_c = lax.optimization_barrier((octet, round_three, theirs_c))
    weight = ordered(octet, round_three, "dp", 8).reshape(-1, width)

    theirs, squares = zip(theirs_a, theirs_b, theirs_c)
    received = exchange(project(theirs, squares, weight, gains), "tensor", 1)
    mine, _, share = attend(core, 0, half, weight, gains)
    received, share = lax.optimization_barrier((received, share))
    parts = lax.all_to_all(
        together(share, received), "tensor", split_axis=0, concat_axis=0, tiled=True,
        axis_index_groups=chips,
    )
    copies = derive(parts, targets, norm_gain.shape[0], total_tokens)
    my_slopes = lax.all_to_all(
        copies, "tensor", split_axis=0, concat_axis=0, tiled=True, axis_index_groups=chips
    )
    their_slopes = exchange(my_slopes, "tensor", 1)
    partial = gradient(my_slopes, (mine,), gains)
    partial = gradient(their_slopes, theirs, gains, partial)
    shares = partial.reshape(lax.axis_size("dp"), -1, width).astype(F16)
    shares = lax.all_to_all(shares, "dp", split_axis=0, concat_axis=0, tiled=True).astype(F32)
    return jnp.sum(shares * jnp.abs(shares), axis=0).T * (1.0 / ROOT_SCALE)


def solution(mesh):
    placed = (
        P("dp", "tensor"),
        P("dp", None),
        P("dp", None),
        P("dp"),
        P(),
        P("tensor", "dp"),
        P(("dp", "tensor"), None),
    )
    return jax.shard_map(
        on_device, mesh=mesh, in_specs=placed, out_specs=P("tensor", "dp"), check_vma=False
    )
```

```python
import math

import jax
import jax.numpy as jnp
from jax import lax
from jax.experimental import pallas as pl
from jax.experimental.pallas import tpu as pltpu
from jax.sharding import PartitionSpec as P

HEADS = 64
KV_HEADS = 8
HEAD_DIM = 128
DOC_MAX = 512
BLOCK = 128
EXTRA = 16
BF16 = jnp.bfloat16
F32 = jnp.float32
F16 = jnp.float16
ROOT_SCALE = 2.0**20


ROOM = pltpu.CompilerParams(vmem_limit_bytes=24 << 20)
IN_VMEM = pl.BlockSpec(memory_space=pltpu.VMEM)


def in_vmem(*arrays):
    return [pltpu.with_memory_space_constraint(x, pltpu.VMEM) for x in arrays]


def scalar_rows(x):
    rows = lax.broadcasted_iota(jnp.int32, (EXTRA, BLOCK), 0)
    high = x.astype(BF16).astype(F32)
    rest = x - high
    middle = rest.astype(BF16).astype(F32)
    low = rest - middle
    return jnp.where(
        rows == 0, high, jnp.where(rows == 1, middle, jnp.where(rows == 2, low, 0.0))
    ).astype(BF16)


def scalar_of(rows):
    return jnp.sum(rows.astype(F32), axis=0, keepdims=True)


def attention(
    places, segment_ids, first, count, query_rows, keys, values, segments
):
    length, width = query_rows.shape
    heads = width // HEAD_DIM
    blocks = length // BLOCK
    most = min(blocks, DOC_MAX // BLOCK + 1)
    step = math.log2(math.e) * HEAD_DIM ** (-0.5)

    def body(place, ids, *refs):
        query, key, value, segment = refs[:4]
        out, square = refs[-2:]
        at = pl.program_id(0)
        block = (first + at) * 2 + place[0]
        needed = 1
        for back in range(1, most):
            end = jnp.maximum((block - back) * BLOCK + BLOCK - 1, 0)
            reached = (block >= back) & (ids[end] == ids[block * BLOCK])
            needed = needed + reached.astype(jnp.int32)

        def over(near):
            window = near * BLOCK
            begin = jnp.maximum(block + 1 - near, 0)
            start = pl.multiple_of(begin * BLOCK, BLOCK)
            shape = (BLOCK, BLOCK)
            diagonal = lax.broadcasted_iota(jnp.int32, shape, 0) == lax.broadcasted_iota(
                jnp.int32, shape, 1
            )
            ones = jnp.ones(shape, BF16)
            columns = [
                jnp.dot(
                    jnp.where(diagonal, segment[pl.ds(begin + n, 1), :], 0)
                    .astype(F32).astype(BF16),
                    ones, preferred_element_type=F32,
                )
                for n in range(near)
            ]
            key_at = start + lax.broadcasted_iota(jnp.int32, (window, BLOCK), 0)
            query_at = block * BLOCK + lax.broadcasted_iota(jnp.int32, (window, BLOCK), 1)
            mine = segment[pl.ds(block, 1), :].astype(F32)
            same = jnp.concatenate(columns, axis=0) == mine
            bias = jnp.where(same & (key_at <= query_at), 0.0, -1e30)
            stacked = jnp.concatenate(
                [query[:, h * HEAD_DIM : (h + 1) * HEAD_DIM] for h in range(heads)], axis=0
            )
            scores = lax.dot_general(
                key[pl.ds(start, window), :], stacked, (((1,), (1,)), ((), ())),
                preferred_element_type=F32,
            )
            scores = scores + jnp.concatenate([bias] * heads, axis=1)
            top = jnp.max(scores, axis=0, keepdims=True)
            shifted = jnp.exp2((scores - top) * step)
            inverse = 1.0 / jnp.sum(shifted, axis=0, keepdims=True)
            probs = (shifted * inverse).astype(BF16)
            mixed = lax.dot_general(
                value[pl.ds(start, window), :], probs, (((0,), (0,)), ((), ())),
                preferred_element_type=F32,
            ).astype(BF16)
            for h in range(heads):
                out[at, h * HEAD_DIM : (h + 1) * HEAD_DIM, :] = mixed[:, h * BLOCK : (h + 1) * BLOCK]

        below = 0
        for near in range(2, most + 1):
            fits = (needed <= near) & (needed > below) if near < most else needed > below
            pl.when(fits)(lambda near=near: over(near))
            below = near

        wide = out[at].astype(F32)
        total = jnp.sum(wide * wide, axis=0, keepdims=True)
        square[at] = jnp.broadcast_to(total, (8, BLOCK))

    in_specs = [pl.BlockSpec((BLOCK, width), lambda i, s, d: ((first + i) * 2 + s[0], 0))]
    out_shape = [
        pltpu.VMEM((count, width, BLOCK), BF16),
        pltpu.VMEM((count, 8, BLOCK), F32),
    ]
    operands = [query_rows, *in_vmem(keys, values), segments]
    grid = pltpu.PrefetchScalarGridSpec(
        num_scalar_prefetch=2,
        grid=(count,),
        in_specs=in_specs + [IN_VMEM] * (len(operands) - 1),
        out_specs=[IN_VMEM] * len(out_shape),
    )
    return pl.pallas_call(body, grid_spec=grid, out_shape=out_shape, name="attention",
        compiler_params=ROOM,
    )(
        places, segment_ids, *operands
    )


def project(attended, squares, weight, gains, kind):
    outs = weight.shape[0]
    rows = outs + EXTRA
    pieces = len(attended)
    count = sum(x.shape[0] for x in attended)

    def body(*refs):
        mat, gain, out = refs[2 * pieces], refs[2 * pieces + 1], refs[-1]
        at = 0
        for att, sq in zip(refs[:pieces], refs[pieces : 2 * pieces]):
            number = att.shape[0]
            wide = jnp.concatenate(
                [(att[u].astype(F32) * gain[...]).astype(BF16) for u in range(number)], axis=1
            )
            sums = jnp.dot(mat[...], wide, preferred_element_type=F32)
            for u in range(number):
                out[at + u, 0:outs, :] = sums[:, u * BLOCK : (u + 1) * BLOCK].astype(kind)
                if kind == F32:
                    out[at + u, outs:rows, :] = jnp.broadcast_to(sq[u, 0:1, :], (EXTRA, BLOCK))
                else:
                    out[at + u, outs:rows, :] = scalar_rows(sq[u, 0:1, :])
            at = at + number

    operands = list(attended) + list(squares) + [weight, gains]
    return pl.pallas_call(
        body,
        in_specs=[IN_VMEM] * len(operands),
        out_specs=IN_VMEM,
        out_shape=pltpu.VMEM((count, rows, BLOCK), kind),
        name="project",
        compiler_params=ROOM,
    )(*in_vmem(*operands))


def together(own, other):
    count, rows, _ = own.shape
    outs = rows - EXTRA

    def body(left, right, out):
        for u in range(count):
            out[u, 0:outs, :] = (
                left[u, 0:outs, :] + right[u, 0:outs, :].astype(F32)
            ).astype(BF16)
            total = left[u, outs : outs + 1, :] + scalar_of(right[u, outs:rows, :])
            out[u, outs:rows, :] = scalar_rows(total)

    return pl.pallas_call(
        body,
        in_specs=[IN_VMEM, IN_VMEM],
        out_specs=IN_VMEM,
        out_shape=pltpu.VMEM(other.shape, BF16),
        name="together",
        compiler_params=ROOM,
    )(*in_vmem(own, other))


def derive(parts, targets, features, total_tokens):
    count, rows, _ = parts.shape
    outs = rows - EXTRA
    root = math.sqrt(total_tokens)

    def body(got, want, out):
        total = jnp.zeros((1, BLOCK), F32)
        sums = jnp.zeros((outs, BLOCK), F32)
        for u in range(count):
            total = total + scalar_of(got[u, outs:rows, :])
            sums = sums + got[u, 0:outs, :].astype(F32)
        factor = lax.rsqrt(total / features + 1e-06)
        residual = sums * factor - want[...].astype(F32).T
        slope = (jnp.clip(residual, -1.0, 1.0) / root).astype(BF16)
        extra = scalar_rows(factor)
        for u in range(count):
            out[u, 0:outs, :] = slope
            out[u, outs:rows, :] = extra

    return pl.pallas_call(
        body,
        in_specs=[IN_VMEM, IN_VMEM],
        out_specs=IN_VMEM,
        out_shape=pltpu.VMEM(parts.shape, BF16),
        name="derive",
        compiler_params=ROOM,
    )(*in_vmem(parts, targets))


def gradient(slopes, attended, gains, before=None):
    count, rows, _ = slopes.shape
    outs = rows - EXTRA
    width = attended[0].shape[1]

    def body(*refs):
        slope, gain = refs[0], refs[1]
        out = refs[-1]
        normed = []
        for att in refs[2 : 2 + len(attended)]:
            for u in range(att.shape[0]):
                factor = scalar_of(slope[len(normed), outs:rows, :])
                normed.append((att[u].astype(F32) * factor * gain[...]).astype(BF16))
        left = jnp.concatenate([slope[u, 0:outs, :] for u in range(count)], axis=1)
        sums = lax.dot_general(
            left, jnp.concatenate(normed, axis=1), (((1,), (1,)), ((), ())),
            preferred_element_type=F32,
        )
        if before is None:
            out[...] = sums
        else:
            sums = sums + refs[-2][...]
            root = jnp.sqrt(jnp.abs(sums) * ROOT_SCALE)
            out[...] = jnp.where(sums < 0, -root, root)

    operands = [slopes, gains] + list(attended) + ([] if before is None else [before])
    return pl.pallas_call(
        body,
        in_specs=[IN_VMEM] * len(operands),
        out_specs=IN_VMEM,
        out_shape=pltpu.VMEM((outs, width), F32),
        name="gradient",
        compiler_params=ROOM,
    )(*in_vmem(*operands))


def exchange(x, axis, bit):
    size = lax.axis_size(axis)
    return lax.ppermute(x, axis, [(i, i ^ bit) for i in range(size)])


def exchanges(x, low, high):
    return (
        x, exchange(x, "dp", low), exchange(x, "dp", high), exchange(x, "dp", low | high)
    )


def joined(pieces, bits):
    size, columns, width = pieces[0].shape
    place = lax.axis_index("dp").astype(jnp.int32).reshape(1)

    def body(at, *refs):
        out = refs[-1]
        own = sum(jnp.where((at[0] & bit) != 0, 1 << n, 0) for n, bit in enumerate(bits))
        for j, piece in enumerate(refs[:-1]):
            out[pl.ds((own ^ j) * size, size)] = piece[...]

    return pl.pallas_call(
        body,
        grid_spec=pltpu.PrefetchScalarGridSpec(
            num_scalar_prefetch=1, grid=(1,), in_specs=[IN_VMEM] * len(pieces), out_specs=IN_VMEM
        ),
        out_shape=pltpu.VMEM((size * len(pieces), columns, width), BF16),
        name="joined",
        compiler_params=ROOM,
    )(place, *in_vmem(*pieces))


def gain_rows(norm_gain, width):
    place = lax.axis_index("tensor").astype(jnp.int32).reshape(1)
    count = width // BLOCK

    def body(at, gain, out):
        for n in range(count):
            row = gain[pl.ds(at[0] * count + n, 1), :]
            out[n * BLOCK : (n + 1) * BLOCK, :] = jnp.broadcast_to(row, (BLOCK, BLOCK)).T

    return pl.pallas_call(
        body,
        grid_spec=pltpu.PrefetchScalarGridSpec(
            num_scalar_prefetch=1, grid=(1,), in_specs=[IN_VMEM], out_specs=IN_VMEM
        ),
        out_shape=pltpu.VMEM((width, BLOCK), F32),
        name="gain_rows",
        compiler_params=ROOM,
    )(place, norm_gain.reshape(-1, BLOCK))


def on_device(query_rows, key_rows, value_rows, segment_ids, norm_gain, draft_weight, targets):
    length, width = query_rows.shape
    blocks = length // BLOCK
    devices = lax.axis_size("tensor")
    total_tokens = length * lax.axis_size("dp")
    place = lax.axis_index("tensor")
    core = place % 2
    chips = [[2 * k + c for k in range(devices // 2)] for c in range(2)]
    kv_head = place * (width // HEAD_DIM) // (HEADS // KV_HEADS)

    segments = segment_ids.reshape(blocks, BLOCK)
    keys = lax.dynamic_slice_in_dim(key_rows, kv_head * HEAD_DIM, HEAD_DIM, 1)
    values = lax.dynamic_slice_in_dim(value_rows, kv_head * HEAD_DIM, HEAD_DIM, 1)
    gains = gain_rows(norm_gain, width)

    def attend(parity, first, count):
        places = parity.astype(jnp.int32).reshape(1)
        return attention(
            places, segment_ids, first, count, query_rows, keys, values, segments
        )

    half = blocks // 2
    cut, last = half // 8, 3 * half // 4
    round_one = exchanges(draft_weight.T[None], 1, 2)
    theirs_a = attend(1 - core, 0, cut)
    round_one, theirs_a = lax.optimization_barrier((round_one, theirs_a))
    quarter = joined(round_one, (1, 2))
    round_two = exchange(quarter, "dp", 4)
    theirs_b = attend(1 - core, cut, half - cut)
    quarter, round_two, theirs_b = lax.optimization_barrier((quarter, round_two, theirs_b))
    octet = joined((quarter, round_two), (4,))
    round_three = exchange(octet, "dp", 8)
    mine_a = attend(core, 0, last)
    octet, round_three, mine_a = lax.optimization_barrier((octet, round_three, mine_a))
    weight = joined((octet, round_three), (8,)).reshape(-1, width)

    theirs, squares = zip(theirs_a, theirs_b)
    received = exchange(project(theirs, squares, weight, gains, BF16), "tensor", 1)
    mine_b = attend(core, last, half - last)
    mine, squares = zip(mine_a, mine_b)
    share = project(mine, squares, weight, gains, F32)
    received, share = lax.optimization_barrier((received, share))
    parts = lax.all_to_all(
        together(share, received), "tensor", split_axis=0, concat_axis=0, tiled=True,
        axis_index_groups=chips,
    )
    copies = derive(parts, targets, norm_gain.shape[0], total_tokens)
    my_slopes = lax.all_to_all(
        copies, "tensor", split_axis=0, concat_axis=0, tiled=True, axis_index_groups=chips
    )
    their_slopes = exchange(my_slopes, "tensor", 1)
    partial = gradient(my_slopes, mine, gains)
    partial = gradient(their_slopes, theirs, gains, partial)
    shares = partial.reshape(lax.axis_size("dp"), -1, width).astype(F16)
    shares = lax.all_to_all(shares, "dp", split_axis=0, concat_axis=0, tiled=True).astype(F32)
    return jnp.sum(shares * jnp.abs(shares), axis=0).T * (1.0 / ROOT_SCALE)


def solution(mesh):
    placed = (
        P("dp", "tensor"),
        P("dp", None),
        P("dp", None),
        P("dp"),
        P(),
        P("tensor", "dp"),
        P(("dp", "tensor"), None),
    )
    return jax.shard_map(
        on_device, mesh=mesh, in_specs=placed, out_specs=P("tensor", "dp"), check_vma=False
    )
```

```python
import math

import jax
import jax.numpy as jnp
from jax import lax
from jax.experimental import pallas as pl
from jax.experimental.pallas import tpu as pltpu
from jax.sharding import PartitionSpec as P

HEADS = 64
KV_HEADS = 8
HEAD_DIM = 128
DOC_MAX = 512
BLOCK = 128
EXTRA = 16
BF16 = jnp.bfloat16
F32 = jnp.float32
F16 = jnp.float16
ROOT_SCALE = 2.0**20


ROOM = pltpu.CompilerParams(vmem_limit_bytes=24 << 20)
IN_VMEM = pl.BlockSpec(memory_space=pltpu.VMEM)


def in_vmem(*arrays):
    return [pltpu.with_memory_space_constraint(x, pltpu.VMEM) for x in arrays]


def scalar_rows(x):
    rows = lax.broadcasted_iota(jnp.int32, (EXTRA, BLOCK), 0)
    high = x.astype(BF16).astype(F32)
    rest = x - high
    middle = rest.astype(BF16).astype(F32)
    low = rest - middle
    return jnp.where(
        rows == 0, high, jnp.where(rows == 1, middle, jnp.where(rows == 2, low, 0.0))
    ).astype(BF16)


def scalar_of(rows):
    return jnp.sum(rows.astype(F32), axis=0, keepdims=True)


def attention(
    places, segment_ids, first, count, query_rows, keys, values, segments
):
    length, width = query_rows.shape
    heads = width // HEAD_DIM
    side = heads
    blocks = length // BLOCK
    most = min(blocks, DOC_MAX // BLOCK + 1)
    step = math.log2(math.e) * HEAD_DIM ** (-0.5)

    def body(place, ids, *refs):
        query, key, value, segment = refs[:4]
        out = refs[-1]
        at = pl.program_id(0)
        block = (first + at) * 2 + place[0]
        needed = 1
        for back in range(1, most):
            end = jnp.maximum((block - back) * BLOCK + BLOCK - 1, 0)
            reached = (block >= back) & (ids[end] == ids[block * BLOCK])
            needed = needed + reached.astype(jnp.int32)

        def over(near):
            window = near * BLOCK
            begin = jnp.maximum(block + 1 - near, 0)
            start = pl.multiple_of(begin * BLOCK, BLOCK)
            shape = (BLOCK, BLOCK)
            diagonal = lax.broadcasted_iota(jnp.int32, shape, 0) == lax.broadcasted_iota(
                jnp.int32, shape, 1
            )
            ones = jnp.ones(shape, BF16)
            columns = [
                jnp.dot(
                    jnp.where(diagonal, segment[pl.ds(begin + n, 1), :], 0)
                    .astype(F32).astype(BF16),
                    ones, preferred_element_type=F32,
                )
                for n in range(near)
            ]
            key_at = start + lax.broadcasted_iota(jnp.int32, (window, BLOCK), 0)
            query_at = block * BLOCK + lax.broadcasted_iota(jnp.int32, (window, BLOCK), 1)
            mine = segment[pl.ds(block, 1), :].astype(F32)
            same = jnp.concatenate(columns, axis=0) == mine
            bias = jnp.where(same & (key_at <= query_at), 0.0, -1e30)
            bias = jnp.concatenate([bias] * side, axis=1)
            near_keys, near_values = key[pl.ds(start, window), :], value[pl.ds(start, window), :]
            for h in range(0, heads, side):
                stacked = jnp.concatenate(
                    [query[:, n * HEAD_DIM : (n + 1) * HEAD_DIM] for n in range(h, h + side)],
                    axis=0,
                )
                scores = bias + lax.dot_general(
                    near_keys, stacked, (((1,), (1,)), ((), ())), preferred_element_type=F32
                )
                top = jnp.max(scores, axis=0, keepdims=True)
                shifted = jnp.exp2((scores - top) * step)
                inverse = 1.0 / jnp.sum(shifted, axis=0, keepdims=True)
                probs = (shifted * inverse).astype(BF16)
                mixed = lax.dot_general(
                    near_values, probs, (((0,), (0,)), ((), ())), preferred_element_type=F32
                ).astype(BF16)
                for n in range(side):
                    out[at, (h + n) * HEAD_DIM : (h + n + 1) * HEAD_DIM, :] = mixed[
                        :, n * BLOCK : (n + 1) * BLOCK
                    ]

        below = 0
        for near in range(2, most + 1):
            fits = (needed <= near) & (needed > below) if near < most else needed > below
            pl.when(fits)(lambda near=near: over(near))
            below = near

    in_specs = [pl.BlockSpec((BLOCK, width), lambda i, s, d: ((first + i) * 2 + s[0], 0))]
    out_shape = pltpu.VMEM((count, width, BLOCK), BF16)
    operands = [query_rows, *in_vmem(keys, values), segments]
    grid = pltpu.PrefetchScalarGridSpec(
        num_scalar_prefetch=2,
        grid=(count,),
        in_specs=in_specs + [IN_VMEM] * (len(operands) - 1),
        out_specs=IN_VMEM,
    )
    return pl.pallas_call(body, grid_spec=grid, out_shape=out_shape, name="attention",
        compiler_params=ROOM,
    )(
        places, segment_ids, *operands
    )


def project(attended, weight, gains, kind):
    outs = weight.shape[0]
    rows = outs + EXTRA
    pieces = len(attended)
    count = sum(x.shape[0] for x in attended)

    def body(*refs):
        mat, gain, out = refs[pieces], refs[pieces + 1], refs[-1]
        at = 0
        for att in refs[:pieces]:
            number = att.shape[0]
            wide = [att[u].astype(F32) for u in range(number)]
            scaled = jnp.concatenate([(x * gain[...]).astype(BF16) for x in wide], axis=1)
            sums = jnp.dot(mat[...], scaled, preferred_element_type=F32)
            for u in range(number):
                out[at + u, 0:outs, :] = sums[:, u * BLOCK : (u + 1) * BLOCK].astype(kind)
                total = jnp.sum(wide[u] * wide[u], axis=0, keepdims=True)
                if kind == F32:
                    out[at + u, outs:rows, :] = jnp.broadcast_to(total, (EXTRA, BLOCK))
                else:
                    out[at + u, outs:rows, :] = scalar_rows(total)
            at = at + number

    operands = list(attended) + [weight, gains]
    return pl.pallas_call(
        body,
        in_specs=[IN_VMEM] * len(operands),
        out_specs=IN_VMEM,
        out_shape=pltpu.VMEM((count, rows, BLOCK), kind),
        name="project",
        compiler_params=ROOM,
    )(*in_vmem(*operands))


def together(own, other):
    count, rows, _ = own.shape
    outs = rows - EXTRA

    def body(left, right, out):
        for u in range(count):
            out[u, 0:outs, :] = (
                left[u, 0:outs, :] + right[u, 0:outs, :].astype(F32)
            ).astype(BF16)
            total = left[u, outs : outs + 1, :] + scalar_of(right[u, outs:rows, :])
            out[u, outs:rows, :] = scalar_rows(total)

    return pl.pallas_call(
        body,
        in_specs=[IN_VMEM, IN_VMEM],
        out_specs=IN_VMEM,
        out_shape=pltpu.VMEM(other.shape, BF16),
        name="together",
        compiler_params=ROOM,
    )(*in_vmem(own, other))


def derive(parts, targets, features, total_tokens):
    count, rows, _ = parts.shape
    outs = rows - EXTRA
    root = math.sqrt(total_tokens)

    def body(got, want, out):
        total = jnp.zeros((1, BLOCK), F32)
        sums = jnp.zeros((outs, BLOCK), F32)
        for u in range(count):
            total = total + scalar_of(got[u, outs:rows, :])
            sums = sums + got[u, 0:outs, :].astype(F32)
        factor = lax.rsqrt(total / features + 1e-06)
        residual = sums * factor - want[...].astype(F32).T
        slope = (jnp.clip(residual, -1.0, 1.0) / root).astype(BF16)
        extra = scalar_rows(factor)
        for u in range(count):
            out[u, 0:outs, :] = slope
            out[u, outs:rows, :] = extra

    return pl.pallas_call(
        body,
        in_specs=[IN_VMEM, IN_VMEM],
        out_specs=IN_VMEM,
        out_shape=pltpu.VMEM(parts.shape, BF16),
        name="derive",
        compiler_params=ROOM,
    )(*in_vmem(parts, targets))


def gradient(slopes, attended, gains, before=None):
    count, rows, _ = slopes.shape
    outs = rows - EXTRA
    width = attended[0].shape[1]

    def body(*refs):
        slope, gain = refs[0], refs[1]
        out = refs[-1]
        normed = []
        for att in refs[2 : 2 + len(attended)]:
            for u in range(att.shape[0]):
                factor = scalar_of(slope[len(normed), outs:rows, :])
                normed.append((att[u].astype(F32) * factor * gain[...]).astype(BF16))
        left = jnp.concatenate([slope[u, 0:outs, :] for u in range(count)], axis=1)
        sums = lax.dot_general(
            left, jnp.concatenate(normed, axis=1), (((1,), (1,)), ((), ())),
            preferred_element_type=F32,
        )
        if before is None:
            out[...] = sums
        else:
            sums = sums + refs[-2][...]
            root = jnp.sqrt(jnp.abs(sums) * ROOT_SCALE)
            out[...] = jnp.where(sums < 0, -root, root)

    operands = [slopes, gains] + list(attended) + ([] if before is None else [before])
    return pl.pallas_call(
        body,
        in_specs=[IN_VMEM] * len(operands),
        out_specs=IN_VMEM,
        out_shape=pltpu.VMEM((outs, width), F32),
        name="gradient",
        compiler_params=ROOM,
    )(*in_vmem(*operands))


def exchange(x, axis, bit):
    size = lax.axis_size(axis)
    return lax.ppermute(x, axis, [(i, i ^ bit) for i in range(size)])


def exchanges(x, low, high):
    return (
        x, exchange(x, "dp", low), exchange(x, "dp", high), exchange(x, "dp", low | high)
    )


def joined(pieces, bits):
    size, columns, width = pieces[0].shape
    place = lax.axis_index("dp").astype(jnp.int32).reshape(1)

    def body(at, *refs):
        out = refs[-1]
        own = sum(jnp.where((at[0] & bit) != 0, 1 << n, 0) for n, bit in enumerate(bits))
        for j, piece in enumerate(refs[:-1]):
            out[pl.ds((own ^ j) * size, size)] = piece[...]

    return pl.pallas_call(
        body,
        grid_spec=pltpu.PrefetchScalarGridSpec(
            num_scalar_prefetch=1, grid=(1,), in_specs=[IN_VMEM] * len(pieces), out_specs=IN_VMEM
        ),
        out_shape=pltpu.VMEM((size * len(pieces), columns, width), BF16),
        name="joined",
        compiler_params=ROOM,
    )(place, *in_vmem(*pieces))


def gain_rows(norm_gain, width):
    place = lax.axis_index("tensor").astype(jnp.int32).reshape(1)
    count = width // BLOCK

    def body(at, gain, out):
        for n in range(count):
            row = gain[pl.ds(at[0] * count + n, 1), :]
            out[n * BLOCK : (n + 1) * BLOCK, :] = jnp.broadcast_to(row, (BLOCK, BLOCK)).T

    return pl.pallas_call(
        body,
        grid_spec=pltpu.PrefetchScalarGridSpec(
            num_scalar_prefetch=1, grid=(1,), in_specs=[IN_VMEM], out_specs=IN_VMEM
        ),
        out_shape=pltpu.VMEM((width, BLOCK), F32),
        name="gain_rows",
        compiler_params=ROOM,
    )(place, norm_gain.reshape(-1, BLOCK))


def on_device(query_rows, key_rows, value_rows, segment_ids, norm_gain, draft_weight, targets):
    length, width = query_rows.shape
    blocks = length // BLOCK
    devices = lax.axis_size("tensor")
    total_tokens = length * lax.axis_size("dp")
    place = lax.axis_index("tensor")
    core = place % 2
    chips = [[2 * k + c for k in range(devices // 2)] for c in range(2)]
    kv_head = place * (width // HEAD_DIM) // (HEADS // KV_HEADS)

    segments = segment_ids.reshape(blocks, BLOCK)
    keys = lax.dynamic_slice_in_dim(key_rows, kv_head * HEAD_DIM, HEAD_DIM, 1)
    values = lax.dynamic_slice_in_dim(value_rows, kv_head * HEAD_DIM, HEAD_DIM, 1)
    gains = gain_rows(norm_gain, width)

    def attend(parity, first, count):
        places = parity.astype(jnp.int32).reshape(1)
        return attention(
            places, segment_ids, first, count, query_rows, keys, values, segments
        )

    half = blocks // 2
    cut, last = half // 8, 3 * half // 4
    round_one = exchanges(draft_weight.T[None], 1, 2)
    theirs_a = attend(1 - core, 0, cut)
    round_one, theirs_a = lax.optimization_barrier((round_one, theirs_a))
    quarter = joined(round_one, (1, 2))
    round_two = exchange(quarter, "dp", 4)
    theirs_b = attend(1 - core, cut, half - cut)
    quarter, round_two, theirs_b = lax.optimization_barrier((quarter, round_two, theirs_b))
    octet = joined((quarter, round_two), (4,))
    round_three = exchange(octet, "dp", 8)
    mine_a = attend(core, 0, last)
    octet, round_three, mine_a = lax.optimization_barrier((octet, round_three, mine_a))
    weight = joined((octet, round_three), (8,)).reshape(-1, width)

    theirs = (theirs_a, theirs_b)
    received = exchange(project(theirs, weight, gains, BF16), "tensor", 1)
    mine = (mine_a, attend(core, last, half - last))
    share = project(mine, weight, gains, F32)
    received, share = lax.optimization_barrier((received, share))
    parts = lax.all_to_all(
        together(share, received), "tensor", split_axis=0, concat_axis=0, tiled=True,
        axis_index_groups=chips,
    )
    copies = derive(parts, targets, norm_gain.shape[0], total_tokens)
    my_slopes = lax.all_to_all(
        copies, "tensor", split_axis=0, concat_axis=0, tiled=True, axis_index_groups=chips
    )
    their_slopes = exchange(my_slopes, "tensor", 1)
    partial = gradient(my_slopes, mine, gains)
    partial = gradient(their_slopes, theirs, gains, partial)
    shares = partial.reshape(lax.axis_size("dp"), -1, width).astype(F16)
    shares = lax.all_to_all(shares, "dp", split_axis=0, concat_axis=0, tiled=True).astype(F32)
    return jnp.sum(shares * jnp.abs(shares), axis=0).T * (1.0 / ROOT_SCALE)


def solution(mesh):
    placed = (
        P("dp", "tensor"),
        P("dp", None),
        P("dp", None),
        P("dp"),
        P(),
        P("tensor", "dp"),
        P(("dp", "tensor"), None),
    )
    return jax.shard_map(
        on_device, mesh=mesh, in_specs=placed, out_specs=P("tensor", "dp"), check_vma=False
    )
```

```python
import math

import jax
import jax.numpy as jnp
from jax import lax
from jax.experimental import pallas as pl
from jax.experimental.pallas import tpu as pltpu
from jax.sharding import PartitionSpec as P

HEADS = 64
KV_HEADS = 8
HEAD_DIM = 128
DOC_MAX = 512
BLOCK = 128
EXTRA = 16
BF16 = jnp.bfloat16
F32 = jnp.float32
F16 = jnp.float16
RING = 8
ROOT_SCALE = 2.0**20


ROOM = pltpu.CompilerParams(vmem_limit_bytes=24 << 20)
IN_VMEM = pl.BlockSpec(memory_space=pltpu.VMEM)


def in_vmem(*arrays):
    return [pltpu.with_memory_space_constraint(x, pltpu.VMEM) for x in arrays]


def scalar_rows(x):
    rows = lax.broadcasted_iota(jnp.int32, (EXTRA, BLOCK), 0)
    high = x.astype(BF16).astype(F32)
    rest = x - high
    middle = rest.astype(BF16).astype(F32)
    low = rest - middle
    return jnp.where(
        rows == 0, high, jnp.where(rows == 1, middle, jnp.where(rows == 2, low, 0.0))
    ).astype(BF16)


def scalar_of(rows):
    return jnp.sum(rows.astype(F32), axis=0, keepdims=True)


def attention(
    places, segment_ids, first, count, query_rows, keys, values, segments
):
    length, width = query_rows.shape
    heads = width // HEAD_DIM
    side = heads
    blocks = length // BLOCK
    most = min(blocks, DOC_MAX // BLOCK + 1)
    step = math.log2(math.e) * HEAD_DIM ** (-0.5)

    def body(place, ids, *refs):
        query, key, value, segment = refs[:4]
        out = refs[-1]
        at = pl.program_id(0)
        block = (first + at) * 2 + place[0]
        needed = 1
        for back in range(1, most):
            end = jnp.maximum((block - back) * BLOCK + BLOCK - 1, 0)
            reached = (block >= back) & (ids[end] == ids[block * BLOCK])
            needed = needed + reached.astype(jnp.int32)

        def over(near):
            window = near * BLOCK
            begin = jnp.maximum(block + 1 - near, 0)
            start = pl.multiple_of(begin * BLOCK, BLOCK)
            shape = (BLOCK, BLOCK)
            diagonal = lax.broadcasted_iota(jnp.int32, shape, 0) == lax.broadcasted_iota(
                jnp.int32, shape, 1
            )
            ones = jnp.ones(shape, BF16)
            columns = [
                jnp.dot(
                    jnp.where(diagonal, segment[pl.ds(begin + n, 1), :], 0)
                    .astype(F32).astype(BF16),
                    ones, preferred_element_type=F32,
                )
                for n in range(near)
            ]
            key_at = start + lax.broadcasted_iota(jnp.int32, (window, BLOCK), 0)
            query_at = block * BLOCK + lax.broadcasted_iota(jnp.int32, (window, BLOCK), 1)
            mine = segment[pl.ds(block, 1), :].astype(F32)
            same = jnp.concatenate(columns, axis=0) == mine
            bias = jnp.where(same & (key_at <= query_at), 0.0, -1e30)
            bias = jnp.concatenate([bias] * side, axis=1)
            near_keys, near_values = key[pl.ds(start, window), :], value[pl.ds(start, window), :]
            for h in range(0, heads, side):
                stacked = jnp.concatenate(
                    [query[:, n * HEAD_DIM : (n + 1) * HEAD_DIM] for n in range(h, h + side)],
                    axis=0,
                )
                scores = bias + lax.dot_general(
                    near_keys, stacked, (((1,), (1,)), ((), ())), preferred_element_type=F32
                )
                top = jnp.max(scores, axis=0, keepdims=True)
                shifted = jnp.exp2((scores - top) * step)
                inverse = 1.0 / jnp.sum(shifted, axis=0, keepdims=True)
                probs = (shifted * inverse).astype(BF16)
                mixed = lax.dot_general(
                    near_values, probs, (((0,), (0,)), ((), ())), preferred_element_type=F32
                ).astype(BF16)
                for n in range(side):
                    out[at, (h + n) * HEAD_DIM : (h + n + 1) * HEAD_DIM, :] = mixed[
                        :, n * BLOCK : (n + 1) * BLOCK
                    ]

        below = 0
        for near in range(2, most + 1):
            fits = (needed <= near) & (needed > below) if near < most else needed > below
            pl.when(fits)(lambda near=near: over(near))
            below = near

    in_specs = [pl.BlockSpec((BLOCK, width), lambda i, s, d: ((first + i) * 2 + s[0], 0))]
    out_shape = pltpu.VMEM((count, width, BLOCK), BF16)
    operands = [query_rows, *in_vmem(keys, values), segments]
    grid = pltpu.PrefetchScalarGridSpec(
        num_scalar_prefetch=2,
        grid=(count,),
        in_specs=in_specs + [IN_VMEM] * (len(operands) - 1),
        out_specs=IN_VMEM,
    )
    return pl.pallas_call(body, grid_spec=grid, out_shape=out_shape, name="attention",
        compiler_params=ROOM,
    )(
        places, segment_ids, *operands
    )


def project(attended, weight, gains, kind):
    outs = weight.shape[0]
    rows = outs + EXTRA
    pieces = len(attended)
    count = sum(x.shape[0] for x in attended)

    def body(*refs):
        mat, gain, out = refs[pieces], refs[pieces + 1], refs[-1]
        at = 0
        for att in refs[:pieces]:
            number = att.shape[0]
            wide = [att[u].astype(F32) for u in range(number)]
            scaled = jnp.concatenate([(x * gain[...]).astype(BF16) for x in wide], axis=1)
            sums = jnp.dot(mat[...], scaled, preferred_element_type=F32)
            for u in range(number):
                out[at + u, 0:outs, :] = sums[:, u * BLOCK : (u + 1) * BLOCK].astype(kind)
                total = jnp.sum(wide[u] * wide[u], axis=0, keepdims=True)
                if kind == F32:
                    out[at + u, outs:rows, :] = jnp.broadcast_to(total, (EXTRA, BLOCK))
                else:
                    out[at + u, outs:rows, :] = scalar_rows(total)
            at = at + number

    operands = list(attended) + [weight, gains]
    return pl.pallas_call(
        body,
        in_specs=[IN_VMEM] * len(operands),
        out_specs=IN_VMEM,
        out_shape=pltpu.VMEM((count, rows, BLOCK), kind),
        name="project",
        compiler_params=ROOM,
    )(*in_vmem(*operands))


def together(own, other):
    count, rows, _ = own.shape
    outs = rows - EXTRA

    def body(left, right, out):
        for u in range(count):
            out[u, 0:outs, :] = (
                left[u, 0:outs, :] + right[u, 0:outs, :].astype(F32)
            ).astype(BF16)
            total = left[u, outs : outs + 1, :] + scalar_of(right[u, outs:rows, :])
            out[u, outs:rows, :] = scalar_rows(total)

    return pl.pallas_call(
        body,
        in_specs=[IN_VMEM, IN_VMEM],
        out_specs=IN_VMEM,
        out_shape=pltpu.VMEM(other.shape, BF16),
        name="together",
        compiler_params=ROOM,
    )(*in_vmem(own, other))


def derive(parts, targets, features, total_tokens):
    count, rows, _ = parts.shape
    outs = rows - EXTRA
    root = math.sqrt(total_tokens)

    def body(got, want, out):
        total = jnp.zeros((1, BLOCK), F32)
        sums = jnp.zeros((outs, BLOCK), F32)
        for u in range(count):
            total = total + scalar_of(got[u, outs:rows, :])
            sums = sums + got[u, 0:outs, :].astype(F32)
        factor = lax.rsqrt(total / features + 1e-06)
        residual = sums * factor - want[...].astype(F32).T
        slope = (jnp.clip(residual, -1.0, 1.0) / root).astype(BF16)
        extra = scalar_rows(factor)
        for u in range(count):
            out[u, 0:outs, :] = slope
            out[u, outs:rows, :] = extra

    return pl.pallas_call(
        body,
        in_specs=[IN_VMEM, IN_VMEM],
        out_specs=IN_VMEM,
        out_shape=pltpu.VMEM(parts.shape, BF16),
        name="derive",
        compiler_params=ROOM,
    )(*in_vmem(parts, targets))


def gradient(slopes, attended, gains, before=None):
    count, rows, _ = slopes.shape
    outs = rows - EXTRA
    width = attended[0].shape[1]

    def body(*refs):
        slope, gain = refs[0], refs[1]
        out = refs[-1]
        normed = []
        for att in refs[2 : 2 + len(attended)]:
            for u in range(att.shape[0]):
                factor = scalar_of(slope[len(normed), outs:rows, :])
                normed.append((att[u].astype(F32) * factor * gain[...]).astype(BF16))
        left = jnp.concatenate([slope[u, 0:outs, :] for u in range(count)], axis=1)
        sums = lax.dot_general(
            left, jnp.concatenate(normed, axis=1), (((1,), (1,)), ((), ())),
            preferred_element_type=F32,
        )
        if before is None:
            out[...] = sums
        else:
            sums = sums + refs[-2][...]
            root = jnp.sqrt(jnp.abs(sums) * ROOT_SCALE)
            out[...] = jnp.where(sums < 0, -root, root)

    operands = [slopes, gains] + list(attended) + ([] if before is None else [before])
    return pl.pallas_call(
        body,
        in_specs=[IN_VMEM] * len(operands),
        out_specs=IN_VMEM,
        out_shape=pltpu.VMEM((outs, width), F32),
        name="gradient",
        compiler_params=ROOM,
    )(*in_vmem(*operands))


def exchange(x, axis, bit):
    size = lax.axis_size(axis)
    return lax.ppermute(x, axis, [(i, i ^ bit) for i in range(size)])


def shifted(x, step):
    size = lax.axis_size("dp")
    return lax.ppermute(
        x, "dp", [(i, i - i % RING + (i - step) % RING) for i in range(size)]
    )


def joined(pieces, slots, count):
    _, columns, width = pieces[0].shape
    place = lax.axis_index("dp").astype(jnp.int32).reshape(1)

    def body(at, *refs):
        out = refs[-1]
        for j, piece in enumerate(refs[:-1]):
            for n, slot in enumerate(slots(at[0], j)):
                out[slot] = piece[n]

    return pl.pallas_call(
        body,
        grid_spec=pltpu.PrefetchScalarGridSpec(
            num_scalar_prefetch=1, grid=(1,), in_specs=[IN_VMEM] * len(pieces), out_specs=IN_VMEM
        ),
        out_shape=pltpu.VMEM((count, columns, width), BF16),
        name="joined",
        compiler_params=ROOM,
    )(place, *in_vmem(*pieces))


def gain_rows(norm_gain, width):
    place = lax.axis_index("tensor").astype(jnp.int32).reshape(1)
    count = width // BLOCK

    def body(at, gain, out):
        for n in range(count):
            row = gain[pl.ds(at[0] * count + n, 1), :]
            out[n * BLOCK : (n + 1) * BLOCK, :] = jnp.broadcast_to(row, (BLOCK, BLOCK)).T

    return pl.pallas_call(
        body,
        grid_spec=pltpu.PrefetchScalarGridSpec(
            num_scalar_prefetch=1, grid=(1,), in_specs=[IN_VMEM], out_specs=IN_VMEM
        ),
        out_shape=pltpu.VMEM((width, BLOCK), F32),
        name="gain_rows",
        compiler_params=ROOM,
    )(place, norm_gain.reshape(-1, BLOCK))


def on_device(query_rows, key_rows, value_rows, segment_ids, norm_gain, draft_weight, targets):
    length, width = query_rows.shape
    blocks = length // BLOCK
    devices = lax.axis_size("tensor")
    total_tokens = length * lax.axis_size("dp")
    place = lax.axis_index("tensor")
    core = place % 2
    chips = [[2 * k + c for k in range(devices // 2)] for c in range(2)]
    kv_head = place * (width // HEAD_DIM) // (HEADS // KV_HEADS)

    segments = segment_ids.reshape(blocks, BLOCK)
    keys = lax.dynamic_slice_in_dim(key_rows, kv_head * HEAD_DIM, HEAD_DIM, 1)
    values = lax.dynamic_slice_in_dim(value_rows, kv_head * HEAD_DIM, HEAD_DIM, 1)
    gains = gain_rows(norm_gain, width)

    def attend(parity, first, count):
        places = parity.astype(jnp.int32).reshape(1)
        return attention(
            places, segment_ids, first, count, query_rows, keys, values, segments
        )

    half = blocks // 2
    cut, last = half // 8, 3 * half // 4
    shard = draft_weight.T[None]
    ahead, behind = shifted(shard, 1), shifted(shard, -1)
    theirs_a = attend(1 - core, 0, cut)
    ahead, behind, theirs_a = lax.optimization_barrier((ahead, behind, theirs_a))
    trio = joined((behind, shard, ahead), lambda place, j: (j,), 3)
    duo = joined((shard, ahead), lambda place, j: (j,), 2)
    far_ahead, far_behind = shifted(trio, 3), shifted(duo, -3)
    theirs_b = attend(1 - core, cut, half - cut)
    trio, far_ahead, far_behind, theirs_b = lax.optimization_barrier(
        (trio, far_ahead, far_behind, theirs_b)
    )
    starts = (RING - 1, 2, RING - 3)
    octet = joined(
        (trio, far_ahead, far_behind),
        lambda place, j: [(place + starts[j] + n) % RING for n in range(3 if j < 2 else 2)],
        RING,
    )
    other = exchange(octet, "dp", RING)
    mine_a = attend(core, 0, last)
    octet, other, mine_a = lax.optimization_barrier((octet, other, mine_a))
    weight = joined(
        (octet, other),
        lambda place, j: [(place // RING ^ j) * RING + n for n in range(RING)],
        2 * RING,
    ).reshape(-1, width)

    theirs = (theirs_a, theirs_b)
    received = exchange(project(theirs, weight, gains, BF16), "tensor", 1)
    mine = (mine_a, attend(core, last, half - last))
    share = project(mine, weight, gains, F32)
    received, share = lax.optimization_barrier((received, share))
    parts = lax.all_to_all(
        together(share, received), "tensor", split_axis=0, concat_axis=0, tiled=True,
        axis_index_groups=chips,
    )
    copies = derive(parts, targets, norm_gain.shape[0], total_tokens)
    my_slopes = lax.all_to_all(
        copies, "tensor", split_axis=0, concat_axis=0, tiled=True, axis_index_groups=chips
    )
    their_slopes = exchange(my_slopes, "tensor", 1)
    partial = gradient(my_slopes, mine, gains)
    partial = gradient(their_slopes, theirs, gains, partial)
    shares = partial.reshape(lax.axis_size("dp"), -1, width).astype(F16)
    shares = lax.all_to_all(shares, "dp", split_axis=0, concat_axis=0, tiled=True).astype(F32)
    return jnp.sum(shares * jnp.abs(shares), axis=0).T * (1.0 / ROOT_SCALE)


def solution(mesh):
    placed = (
        P("dp", "tensor"),
        P("dp", None),
        P("dp", None),
        P("dp"),
        P(),
        P("tensor", "dp"),
        P(("dp", "tensor"), None),
    )
    return jax.shard_map(
        on_device, mesh=mesh, in_specs=placed, out_specs=P("tensor", "dp"), check_vma=False
    )
```
